128 devices in a mesh: dp: 16 (over x, z), fsdp: 8 (over y, core).
Axes of the slice: x: 4, y: 4, z: 4, core: 2. Of those that a mesh axis runs over, the one named last changes fastest.
Arguments:
- inputs: float32 [49152, 768], P(('dp', 'fsdp'))
- encoded: bfloat16 [24576, 768], P(('dp', 'fsdp'))
- cotangent: float32 [49152, 768], P(('dp', 'fsdp')), may hold values from -6 to 6
- scoring: bfloat16 [3072, 768], P(('dp', 'fsdp'))
- weights: bfloat16 [9216, 768], P(('dp', 'fsdp'))
- small_params: bfloat16 [2688], P(('dp', 'fsdp'))
- dec_segments: int32 [128, 384], P(('dp', 'fsdp')), may hold values from 0 to 5, as said below
- enc_segments: int32 [128, 192], P(('dp', 'fsdp')), may hold values from 0 to 5, as said below
Outputs:
- output: float32 [49152, 768], P(('dp', 'fsdp'))
- grad_inputs: float32 [49152, 768], P(('dp', 'fsdp'))
- grad_encoded: float32 [24576, 768], P(('dp', 'fsdp'))
- grad_scoring: float32 [3072, 768], P(('dp', 'fsdp'))
- grad_weights: float32 [9216, 768], P(('dp', 'fsdp'))
- grad_small: float32 [2688], P(('dp', 'fsdp'))
The draws below stay inside these ranges and needn't reach their ends.
Inputs may be any that keep to these rules, and one draw needn't show every extreme that they name: In each row of dec_segments the ids start at 0, never fall, rise by at most 1 from one position to the next and change only at multiples of 64; group 0 holds one sequence of 384 rows. Row g of enc_segments is row g of dec_segments with each block of 64 equal ids shortened to 32 of them: encoder sequence s belongs to decoder sequence s of the same group.
All inputs are finite; a program needn't handle non-finite values.
Results may differ from the reference program's by a relative error of at most 0.025.
Values may be sent and summed in bfloat16 or wider, within the bound.
A program may use at most 192 MiB of HBM per device.

```python
import jax
import jax.numpy as jnp
import numpy as np
from jax import lax

D = 768
H = 12
DH = 64
FF = 2048
BUCKETS = 32
UNIT = 64
NGROUPS = 128
GROUP = 384
ENC_GROUP = 192
TOKENS = 49152
ENCTOK = 24576


def segment_units(key):
    units = GROUP // UNIT
    cuts = jax.random.randint(jax.random.fold_in(key, 11), (NGROUPS, units), 0, 2)
    group_ids = jnp.arange(NGROUPS)[:, None]
    unit_ids = jnp.arange(units)[None, :]
    cuts = jnp.where(unit_ids == 0, 0, cuts)
    cuts = jnp.where(group_ids == 0, 0, cuts)
    cuts = jnp.where((group_ids == 1) & (unit_ids > 0), 1, cuts)
    return jnp.cumsum(cuts, axis=1).astype(jnp.int32)


def draw_dec_segments(key, part):
    return jnp.repeat(segment_units(key), UNIT, axis=1).astype(jnp.int32)


def draw_enc_segments(key, part):
    return jnp.repeat(segment_units(key), UNIT // 2, axis=1).astype(jnp.int32)


def draw_inputs(key, part):
    return jax.random.truncated_normal(jax.random.fold_in(key, 51), -6.0, 6.0, (TOKENS, D), jnp.float32)


def draw_encoded(key, part):
    base = jax.random.truncated_normal(jax.random.fold_in(key, 61), -6.0, 6.0, (ENCTOK, D), jnp.float32)
    return base.astype(jnp.bfloat16)


def draw_scoring(key, part):
    base = jax.random.truncated_normal(jax.random.fold_in(key, 22), -4.0, 4.0, (4 * D, D), jnp.float32)
    return (base * (D * DH ** 0.5) ** (-0.5)).astype(jnp.bfloat16)


def draw_weights(key, part):
    total_rows = 4 * D + 3 * FF
    base = jax.random.truncated_normal(jax.random.fold_in(key, 21), -4.0, 4.0, (total_rows, D), jnp.float32)
    row_ids = jnp.arange(total_rows)[:, None]
    scale = jnp.where(row_ids < 4 * D, 2.5 / D ** 0.5, 1.0 / D ** 0.5)
    scale = jnp.where(row_ids >= 4 * D + 2 * FF, 2.0 / FF ** 0.5, scale)
    return (base * scale).astype(jnp.bfloat16)


def draw_small_params(key, part):
    gains = 1.0 + jax.random.uniform(jax.random.fold_in(key, 31), (3 * D,), jnp.float32, -0.4, 0.4)
    table = jax.random.normal(jax.random.fold_in(key, 32), (BUCKETS * H,), jnp.float32)
    return jnp.concatenate([gains, table]).astype(jnp.bfloat16)


def level_of(rng, dims, cuts, least, top_value):
    def one(position, blocks):
        draws = jax.random.uniform(jax.random.fold_in(jax.random.fold_in(rng, 6), position), (blocks,), jnp.float32, least / len(cuts), top_value / len(cuts))
        return jnp.repeat(jnp.exp(draws), dims[position] // blocks).reshape((-1,) + (1,) * (len(dims) - position - 1))

    level = one(*cuts[0])
    for cut in cuts[1:]:
        level = level * one(*cut)
    return level


def centred(own_key, shape, width, limit, shards=(), kind=jnp.bfloat16):
    array = jax.random.normal(own_key, shape, jnp.float32) * width
    if len(shards) > 0:
        array = level_of(own_key, shape, shards, -0.22, 0.18) * array
    return jnp.clip(array, min=-limit, max=limit).astype(kind)


def setup_inputs(seed: int = 0) -> dict:
    seeds = jax.random.split(jax.random.key(seed), 9)
    return {
        "inputs": draw_inputs(jax.random.fold_in(seeds[8], 71), 0),
        "encoded": draw_encoded(jax.random.fold_in(seeds[8], 71), 0),
        "cotangent": centred(seeds[2], (TOKENS, D), 1.0, 6.0, ((0, 128),), jnp.float32),
        "scoring": draw_scoring(jax.random.fold_in(seeds[8], 71), 0),
        "weights": draw_weights(jax.random.fold_in(seeds[8], 71), 0),
        "small_params": draw_small_params(jax.random.fold_in(seeds[8], 71), 0),
        "dec_segments": draw_dec_segments(jax.random.fold_in(seeds[8], 71), 0),
        "enc_segments": draw_enc_segments(jax.random.fold_in(seeds[8], 71), 0),
    }


BUCKET_EDGES = [int(edge_value) for edge_value in np.ceil(16.0 * 8.0 ** ((np.arange(17, 32) - 16) / 16.0))]
EPSILON = 1e-06
MASKED_SCORE = -1e+30

def bucket_index(distance):
    distance = jnp.maximum(distance, 0)
    far_part = jnp.zeros_like(distance)
    for edge_value in BUCKET_EDGES:
        far_part = far_part + (distance >= edge_value).astype(distance.dtype)
    return jnp.where(distance < 16, distance, 16 + far_part).astype(jnp.int32)

def rms_scale(values, gain):
    mean_square = lax.optimization_barrier(jnp.mean(values * values, axis=-1, keepdims=True))
    return values * lax.rsqrt(mean_square + EPSILON) * gain

def gelu_tanh(values):
    return jax.nn.gelu(values, approximate=True)

def to_half(values):
    return values.astype(jnp.bfloat16)

def rounded_wide(values):
    return lax.optimization_barrier(values.astype(jnp.bfloat16)).astype(jnp.float32)

def dot_plain(left, right):
    return jnp.dot(left, right, preferred_element_type=jnp.float32)

def dot_rows(left, right):
    return jnp.dot(left.T, right, preferred_element_type=jnp.float32)

def dot_cols(left, right):
    return jnp.dot(left, right.T, preferred_element_type=jnp.float32)

def split_heads(values):
    return values.reshape(values.shape[0], H, DH).astype(jnp.float32)

def attend_forward(queries, keys, values, allowed, position_bias):
    scores = jnp.einsum('qhd,khd->hqk', split_heads(queries), split_heads(keys))
    if position_bias is not None:
        scores = scores + position_bias
    scores = jnp.where(allowed[None], scores, MASKED_SCORE)
    row_max = lax.optimization_barrier(jnp.max(scores, axis=-1, keepdims=True))
    log_total = row_max + jnp.log(lax.optimization_barrier(jnp.sum(jnp.exp(scores - row_max), axis=-1, keepdims=True)))
    probs = jnp.where(allowed[None], jnp.exp(scores - log_total), 0.0)
    context = jnp.einsum('hqk,khd->qhd', rounded_wide(probs), split_heads(values))
    return (to_half(context.reshape(queries.shape[0], D)), probs)

def attend_backward(queries, keys, values, probs, context, grad_context):
    grad_heads = split_heads(grad_context)
    grad_values = jnp.einsum('hqk,qhd->khd', rounded_wide(probs), grad_heads)
    grad_probs = jnp.einsum('qhd,khd->hqk', grad_heads, split_heads(values))
    delta_rows = lax.optimization_barrier(jnp.sum(grad_heads * split_heads(context), axis=-1)).T[:, :, None]
    grad_scores = probs * (grad_probs - delta_rows)
    scaled = rounded_wide(grad_scores)
    grad_queries = jnp.einsum('hqk,khd->qhd', scaled, split_heads(keys))
    grad_keys = jnp.einsum('hqk,qhd->khd', scaled, split_heads(queries))
    query_total = queries.shape[0]
    key_total = keys.shape[0]
    return (grad_queries.reshape(query_total, D), grad_keys.reshape(key_total, D), grad_values.reshape(key_total, D), grad_scores)

def reference(inputs, encoded, cotangent, scoring, weights, small_params, dec_segments, enc_segments):
    score_parts = [scoring[index * D:(index + 1) * D] for index in range(4)]
    other_parts = [weights[index * D:(index + 1) * D] for index in range(4)]
    blocks = [score_parts[0], score_parts[1], other_parts[0], other_parts[1], score_parts[2], score_parts[3], other_parts[2], other_parts[3]]
    ffn_base = 4 * D
    gate_rows = weights[ffn_base:ffn_base + FF]
    up_rows = weights[ffn_base + FF:ffn_base + 2 * FF]
    down_rows = weights[ffn_base + 2 * FF:ffn_base + 3 * FF]
    gains = small_params[:3 * D].astype(jnp.float32).reshape(3, D)
    table = small_params[3 * D:].astype(jnp.float32).reshape(BUCKETS, H)
    row_ids = jnp.arange(GROUP)
    distance = row_ids[:, None] - row_ids[None, :]
    buckets = bucket_index(distance)
    position_bias = table.T[:, buckets]

    def one_group(totals, pieces):
        group_in, group_enc, group_cot, group_seg, group_eseg = pieces
        self_allowed = (group_seg[:, None] == group_seg[None, :]) & (distance >= 0)
        cross_allowed = group_seg[:, None] == group_eseg[None, :]
        normed_one = to_half(rms_scale(group_in, gains[0]))
        self_queries = to_half(dot_plain(normed_one, blocks[0]))
        self_keys = to_half(dot_plain(normed_one, blocks[1]))
        self_values = to_half(dot_plain(normed_one, blocks[2]))
        self_context, self_probs = attend_forward(self_queries, self_keys, self_values, self_allowed, position_bias)
        first = group_in + dot_plain(self_context, blocks[3])
        normed_two = to_half(rms_scale(first, gains[1]))
        cross_queries = to_half(dot_plain(normed_two, blocks[4]))
        cross_keys = to_half(dot_plain(group_enc, blocks[5]))
        cross_values = to_half(dot_plain(group_enc, blocks[6]))
        cross_context, cross_probs = attend_forward(cross_queries, cross_keys, cross_values, cross_allowed, None)
        second = first + dot_plain(cross_context, blocks[7])
        normed_three = to_half(rms_scale(second, gains[2]))
        gate_pre = dot_cols(normed_three, gate_rows)
        up_pre = dot_cols(normed_three, up_rows)
        gelu_value, gelu_pull = jax.vjp(gelu_tanh, gate_pre)
        hidden = to_half(gelu_value * up_pre)
        output = second + dot_plain(hidden, down_rows)
        cot_half = to_half(group_cot)
        grad_down = dot_rows(hidden, cot_half)
        grad_hidden = dot_cols(cot_half, down_rows)
        grad_gate = to_half(gelu_pull(grad_hidden * up_pre)[0])
        grad_up = to_half(grad_hidden * gelu_value)
        grad_gate_rows = dot_rows(grad_gate, normed_three)
        grad_up_rows = dot_rows(grad_up, normed_three)
        grad_normed_three = dot_plain(grad_gate, gate_rows) + dot_plain(grad_up, up_rows)
        _, norm_pull = jax.vjp(rms_scale, second, gains[2])
        back_second, grad_gain_three = norm_pull(grad_normed_three)
        grad_second = group_cot + back_second
        second_half = to_half(grad_second)
        grad_cross_out = dot_rows(cross_context, second_half)
        grad_cross_context = to_half(dot_cols(second_half, blocks[7]))
        grad_cross_queries, grad_cross_keys, grad_cross_values, _ = attend_backward(cross_queries, cross_keys, cross_values, cross_probs, cross_context, grad_cross_context)
        cross_query_half = to_half(grad_cross_queries)
        cross_key_half = to_half(grad_cross_keys)
        cross_value_half = to_half(grad_cross_values)
        grad_cross_query = dot_rows(normed_two, cross_query_half)
        grad_cross_key = dot_rows(group_enc, cross_key_half)
        grad_cross_value = dot_rows(group_enc, cross_value_half)
        grad_enc = dot_cols(cross_key_half, blocks[5]) + dot_cols(cross_value_half, blocks[6])
        grad_normed_two = dot_cols(cross_query_half, blocks[4])
        _, norm_pull_two = jax.vjp(rms_scale, first, gains[1])
        back_first, grad_gain_two = norm_pull_two(grad_normed_two)
        grad_first = grad_second + back_first
        first_half = to_half(grad_first)
        grad_self_out = dot_rows(self_context, first_half)
        grad_self_context = to_half(dot_cols(first_half, blocks[3]))
        grad_self_queries, grad_self_keys, grad_self_values, grad_scores = attend_backward(self_queries, self_keys, self_values, self_probs, self_context, grad_self_context)
        flat_buckets = buckets.reshape(-1)
        grad_table = jax.vmap(lambda per_head: jax.ops.segment_sum(per_head.reshape(-1), flat_buckets, num_segments=BUCKETS))(grad_scores).T
        query_half = to_half(grad_self_queries)
        key_half = to_half(grad_self_keys)
        value_half = to_half(grad_self_values)
        grad_query = dot_rows(normed_one, query_half)
        grad_key = dot_rows(normed_one, key_half)
        grad_value = dot_rows(normed_one, value_half)
        grad_normed_one = dot_cols(query_half, blocks[0]) + dot_cols(key_half, blocks[1]) + dot_cols(value_half, blocks[2])
        _, norm_pull_one = jax.vjp(rms_scale, group_in, gains[0])
        back_input, grad_gain_one = norm_pull_one(grad_normed_one)
        grad_in = grad_first + back_input
        grad_scoring = jnp.concatenate([grad_query, grad_key, grad_cross_query, grad_cross_key], axis=0)
        grad_weights = jnp.concatenate([grad_value, grad_self_out, grad_cross_value, grad_cross_out, grad_gate_rows, grad_up_rows, grad_down], axis=0)
        grad_small = jnp.concatenate([grad_gain_one, grad_gain_two, grad_gain_three, grad_table.reshape(-1)])
        return ((totals[0] + grad_scoring, totals[1] + grad_weights, totals[2] + grad_small), (output, grad_in, grad_enc))
    start = (jnp.zeros((4 * D, D), jnp.float32), jnp.zeros((4 * D + 3 * FF, D), jnp.float32), jnp.zeros((3 * D + BUCKETS * H,), jnp.float32))
    pieces = (inputs.reshape(NGROUPS, GROUP, D), encoded.reshape(NGROUPS, ENC_GROUP, D), cotangent.reshape(NGROUPS, GROUP, D), dec_segments, enc_segments)
    (grad_scoring, grad_weights, grad_small), (output, grad_in, grad_enc) = lax.scan(one_group, start, pieces)
    return (output.reshape(TOKENS, D), grad_in.reshape(TOKENS, D), grad_enc.reshape(ENCTOK, D), grad_scoring, grad_weights, grad_small)
```

```python
import jax
import jax.numpy as jnp
import numpy as np
from jax import lax
from jax.experimental import pallas as pl
from jax.experimental.pallas import tpu as pltpu
from jax.sharding import PartitionSpec as P

MESH_ID = pl.DeviceIdType.MESH
D = 768
SC_ROWS = 24
WT_ROWS = 72
RING_ORDERS = ((0, 1, 2), (1, 2, 0), (2, 0, 1))
PART_FULL = (((0, 0, 24), (1, 0, 8)), ((1, 8, 32), (2, 0, 8)), ((1, 40, 32),))
PART_LOW = (((0, 0, 16),), ((1, 8, 16), (2, 0, 8)), ((1, 40, 16),))
PART_HIGH = (((0, 16, 8), (1, 0, 8)), ((1, 24, 16),), ((1, 56, 16),))


def grid_place():
    dp = lax.axis_index("dp")
    fs = lax.axis_index("fsdp")
    return [dp // 4, dp % 4, fs // 2], fs % 2


def device_at(place, core):
    return (place[0] * 4 + place[1], place[2] * 2 + core)


def shifted(place, axis, step):
    moved = list(place)
    moved[axis] = (place[axis] + step + 4) % 4
    return moved


def ring_barrier(place, core):
    barrier = pltpu.get_barrier_semaphore()
    for axis in range(3):
        for step in (1, -1):
            pl.semaphore_signal(
                barrier, inc=1, device_id=device_at(shifted(place, axis, step), core), device_id_type=MESH_ID
            )
    pl.semaphore_signal(barrier, inc=1, device_id=device_at(place, 1 - core), device_id_type=MESH_ID)
    pl.semaphore_wait(barrier, 7)


def gather_kernel(sc_in, wt_in, sm_in, sc_out, wt_out, sm_out, local_sem, send_sem, recv_sem):
    place, core = grid_place()
    ins = (sc_in, wt_in, sm_in)
    outs = (sc_out, wt_out, sm_out)
    local = [
        pltpu.make_async_copy(ins[i], outs[i].at[place[0], place[1], place[2], core], local_sem.at[i])
        for i in range(3)
    ]
    for copy in local:
        copy.start()
    ring_barrier(place, core)
    used = [0]
    sends = []

    def block(piece, index):
        array, first, rows = piece
        return outs[array].at[tuple(index) + (core, pl.ds(first, rows))]

    def push(pieces, index, target, from_input=False):
        got = []
        for piece in pieces:
            slot = used[0]
            used[0] += 1
            dst = block(piece, index)
            src = ins[piece[0]].at[pl.ds(piece[1], piece[2])] if from_input else dst
            copy = pltpu.make_async_remote_copy(
                src_ref=src,
                dst_ref=dst,
                send_sem=send_sem.at[slot],
                recv_sem=recv_sem.at[slot],
                device_id=target,
                device_id_type=MESH_ID,
            )
            copy.start()
            sends.append(copy)
            got.append(copy)
        return got

    def arrive(copies):
        for copy in copies:
            copy.wait_recv()

    sibling = device_at(place, 1 - core)
    cross = []
    for stage in range(3):
        first = []
        for part in range(3):
            order = RING_ORDERS[part]
            axis = order[stage]
            index = [slice(None) if order.index(k) < stage else place[k] for k in range(3)]
            up = push(PART_FULL[part], index, device_at(shifted(place, axis, 1), core), stage == 0)
            down = push(PART_FULL[part], index, device_at(shifted(place, axis, -1), core), stage == 0)
            first.append((axis, index, up, down))
        if stage == 0:
            for part in range(3):
                cross += push(PART_FULL[part], place, sibling, True)
            for copy in local:
                copy.wait()
        second = []
        for part in range(3):
            axis, index, up, down = first[part]
            left = list(index)
            left[axis] = (place[axis] + 3) % 4
            right = list(index)
            right[axis] = (place[axis] + 1) % 4
            arrive(up)
            up2 = push(PART_LOW[part], left, device_at(shifted(place, axis, 1), core))
            cross += push(PART_FULL[part], left, sibling)
            arrive(down)
            down2 = push(PART_HIGH[part], right, device_at(shifted(place, axis, -1), core))
            cross += push(PART_FULL[part], right, sibling)
            second.append((axis, index, up2, down2))
        for part in range(3):
            axis, index, up2, down2 = second[part]
            far = list(index)
            far[axis] = (place[axis] + 2) % 4
            arrive(up2)
            cross += push(PART_LOW[part], far, sibling)
            arrive(down2)
            cross += push(PART_HIGH[part], far, sibling)
    arrive(cross)
    for copy in sends:
        copy.wait_send()


GATHER_COPIES = 5 + 3 * 36


def gather_params(scoring, weights, small):
    small_tile = jnp.pad(small.reshape(1, 21), ((0, 7), (0, 107)))
    any_spec = pl.BlockSpec(memory_space=pl.ANY)
    full_sc, full_wt, full_sm = pl.pallas_call(
        gather_kernel,
        out_shape=(
            jax.ShapeDtypeStruct((4, 4, 4, 2, SC_ROWS, D), jnp.bfloat16),
            jax.ShapeDtypeStruct((4, 4, 4, 2, WT_ROWS, D), jnp.bfloat16),
            jax.ShapeDtypeStruct((4, 4, 4, 2, 8, 128), jnp.bfloat16),
        ),
        in_specs=[any_spec] * 3,
        out_specs=(any_spec,) * 3,
        scratch_shapes=[
            pltpu.SemaphoreType.DMA((3,)),
            pltpu.SemaphoreType.DMA((GATHER_COPIES,)),
            pltpu.SemaphoreType.DMA((GATHER_COPIES,)),
        ],
        compiler_params=pltpu.CompilerParams(collective_id=0, has_side_effects=True),
        name="gather_params",
    )(scoring, weights, small_tile)
    return (
        full_sc.reshape(3072, D),
        full_wt.reshape(9216, D),
        full_sm[..., 0, :21].reshape(2688),
    )


RS_FULL = (((0, 0, 24), (1, 0, 8)), ((1, 8, 32),), ((1, 40, 32),))
RS_LOW = (((0, 0, 16),), ((1, 8, 16),), ((1, 40, 16),))
RS_HIGH = (((0, 16, 8), (1, 0, 8)), ((1, 24, 16),), ((1, 56, 16),))


def scatter_kernel(g_sc, g_wt, g_sm, o_sc, o_wt, o_sm, acc_sc, acc_wt, sib_sc, sib_wt, bufs, small_own, small_in,
                   local_sem, send_sem, recv_sem):
    place, core = grid_place()
    grads = (g_sc, g_wt)
    accs = (acc_sc, acc_wt)
    sibs = (sib_sc, sib_wt)
    used = [0]
    sends = []

    def push(src, dst, target):
        slot = used[0]
        used[0] += 1
        copy = pltpu.make_async_remote_copy(
            src_ref=src, dst_ref=dst, send_sem=send_sem.at[slot], recv_sem=recv_sem.at[slot],
            device_id=target, device_id_type=MESH_ID,
        )
        copy.start()
        sends.append(copy)
        return copy

    sibling = device_at(place, 1 - core)
    pieces0 = [piece for part in RS_FULL for piece in part]
    own = []
    for i, (array, first, rows) in enumerate(pieces0):
        copy = pltpu.make_async_copy(
            grads[array].at[:, :, :, core, pl.ds(first, rows)],
            accs[array].at[:, :, :, pl.ds(first, rows)],
            local_sem.at[i],
        )
        copy.start()
        own.append(copy)
    small_copy = pltpu.make_async_copy(g_sm, small_own, local_sem.at[len(pieces0)])
    small_copy.start()
    ring_barrier(place, core)
    from_sib = []
    for array, first, rows in pieces0:
        from_sib.append(
            push(
                grads[array].at[:, :, :, 1 - core, pl.ds(first, rows)],
                sibs[array].at[:, :, :, pl.ds(first, rows)],
                sibling,
            )
        )
    small_copy.wait()
    small_first = push(small_own, small_in.at[0], sibling)

    def add_all(array, first, rows):
        def body(n, carry):
            a, b, e = n // 16, (n // 4) % 4, n % 4
            here = (a, b, e, pl.ds(first, rows))
            total = accs[array][here].astype(jnp.float32) + sibs[array][here].astype(jnp.float32)
            accs[array][here] = total.astype(jnp.bfloat16)
            return carry

        lax.fori_loop(0, 64, body, 0)

    def acc_at(piece, index):
        array, first, rows = piece
        return accs[array].at[tuple(index) + (pl.ds(first, rows),)]

    def add_into(piece, index, buf, free_axes, final=None):
        array, first, rows = piece
        count = 4 ** len(free_axes)

        def body(n, carry):
            here = list(index)
            local = []
            for position, axis in enumerate(free_axes):
                coord = (n // (4 ** (len(free_axes) - 1 - position))) % 4
                here[axis] = coord
                local.append(coord)
            where = tuple(here) + (pl.ds(first, rows),)
            total = accs[array][where].astype(jnp.float32) + buf[tuple(local) + (slice(None),)].astype(jnp.float32)
            accs[array][where] = total.astype(jnp.bfloat16)
            return carry

        lax.fori_loop(0, count, body, 0)

    buf_at = [0]

    def take_buf():
        buf = bufs[buf_at[0]]
        buf_at[0] += 1
        return buf

    count = 0
    state = {}
    for stage in range(3):
        for part in range(3):
            order = RING_ORDERS[part]
            axis = order[stage]
            free = sorted(order[stage + 1:])
            index = [slice(None) if k in free else place[k] for k in range(3)]
            if stage == 0:
                for piece in RS_FULL[part]:
                    own[count].wait()
                    from_sib[count].wait_recv()
                    add_all(*piece)
                    count += 1
            far = list(index)
            far[axis] = (place[axis] + 2) % 4
            up_dev = device_at(shifted(place, axis, 1), core)
            down_dev = device_at(shifted(place, axis, -1), core)
            low = []
            for piece in RS_LOW[part]:
                buf = take_buf()
                low.append((piece, buf, push(acc_at(piece, far), buf, up_dev)))
            high = []
            for piece in RS_HIGH[part]:
                buf = take_buf()
                high.append((piece, buf, push(acc_at(piece, far), buf, down_dev)))
            state[part] = (axis, free, index, up_dev, down_dev, low, high)
        if stage == 0:
            small_first.wait_recv()
            small_own2 = small_own[...] + small_in[0]
        for part in range(3):
            axis, free, index, up_dev, down_dev, low, high = state[part]
            right = list(index)
            right[axis] = (place[axis] + 1) % 4
            left = list(index)
            left[axis] = (place[axis] + 3) % 4
            for piece, buf, copy in low:
                copy.wait_recv()
                add_into(piece, right, buf, free)
            ups = []
            for piece in RS_FULL[part]:
                buf = take_buf()
                ups.append((piece, buf, push(acc_at(piece, right), buf, up_dev)))
            for piece, buf, copy in high:
                copy.wait_recv()
                add_into(piece, left, buf, free)
            downs = []
            for piece in RS_FULL[part]:
                buf = take_buf()
                downs.append((piece, buf, push(acc_at(piece, left), buf, down_dev)))
            state[part] = (axis, free, index, ups, downs)
        for part in range(3):
            axis, free, index, ups, downs = state[part]
            if stage < 2:
                for piece, buf, copy in ups + downs:
                    copy.wait_recv()
                    add_into(piece, index, buf, free)
            else:
                for (piece, buf, copy), (_, buf2, copy2) in zip(ups, downs):
                    copy.wait_recv()
                    copy2.wait_recv()
                    array, first, rows = piece
                    out = (o_sc, o_wt)[array]
                    out[pl.ds(first, rows)] = (
                        accs[array][tuple(place) + (pl.ds(first, rows),)].astype(jnp.float32)
                        + buf[...].astype(jnp.float32)
                        + buf2[...].astype(jnp.float32)
                    )
    for axis in range(3):
        small_copy_ref = small_in.at[1 + 4 * axis]
        small_copy_ref[...] = small_own2
        got = []
        for k, step in enumerate((1, -1, 2)):
            got.append(
                push(small_copy_ref, small_in.at[2 + 4 * axis + k], device_at(shifted(place, axis, step), core))
            )
        for copy in got:
            copy.wait_recv()
        small_own2 = small_own2 + small_in[2 + 4 * axis] + small_in[3 + 4 * axis] + small_in[4 + 4 * axis]
    o_sm[...] = small_own2
    for copy in sends:
        copy.wait_send()


def rs_buffers():
    shapes = []
    for stage in range(3):
        lead = (4,) * (2 - stage)
        for part in range(3):
            for piece in RS_LOW[part] + RS_HIGH[part]:
                shapes.append(pltpu.VMEM(lead + (piece[2], D), jnp.bfloat16))
        for part in range(3):
            for piece in RS_FULL[part] * 2:
                shapes.append(pltpu.VMEM(lead + (piece[2], D), jnp.bfloat16))
    return shapes


SCATTER_COPIES = 4 + 1 + 3 * (7 + 8) + 9


def scatter_grads(g_sc, g_wt, g_small):
    any_spec = pl.BlockSpec(memory_space=pl.ANY)
    vmem = pl.BlockSpec(memory_space=pltpu.VMEM)
    small = jnp.pad(g_small.reshape(21, 128), ((0, 3), (0, 0)))
    o_sc, o_wt, o_sm = pl.pallas_call(
        scatter_kernel,
        out_shape=(
            jax.ShapeDtypeStruct((SC_ROWS, D), jnp.float32),
            jax.ShapeDtypeStruct((WT_ROWS, D), jnp.float32),
            jax.ShapeDtypeStruct((24, 128), jnp.float32),
        ),
        in_specs=[any_spec] * 3,
        out_specs=(vmem,) * 3,
        scratch_shapes=[
            pltpu.VMEM((4, 4, 4, SC_ROWS, D), jnp.bfloat16),
            pltpu.VMEM((4, 4, 4, WT_ROWS, D), jnp.bfloat16),
            pltpu.VMEM((4, 4, 4, SC_ROWS, D), jnp.bfloat16),
            pltpu.VMEM((4, 4, 4, WT_ROWS, D), jnp.bfloat16),
            rs_buffers(),
            pltpu.VMEM((24, 128), jnp.float32),
            pltpu.VMEM((13, 24, 128), jnp.float32),
            pltpu.SemaphoreType.DMA((5,)),
            pltpu.SemaphoreType.DMA((SCATTER_COPIES,)),
            pltpu.SemaphoreType.DMA((SCATTER_COPIES,)),
        ],
        compiler_params=pltpu.CompilerParams(
            collective_id=1, has_side_effects=True, vmem_limit_bytes=56 << 20
        ),
        name="scatter_grads",
    )(g_sc.reshape(4, 4, 4, 2, SC_ROWS, D), g_wt.reshape(4, 4, 4, 2, WT_ROWS, D), small)
    me = lax.axis_index("dp") * 8 + lax.axis_index("fsdp")
    mine = lax.dynamic_slice(o_sm.reshape(-1), (me * 21,), (21,))
    return o_sc, o_wt, mine
FF = 2048
H = 12
BUCKETS = 32
ROWS = 384
KEYS = 192
PAIRS = 6
CH = 256
SPAN = 640
EPSILON = 1e-06
MASKED_SCORE = -1e30
BUCKET_EDGES = [int(e) for e in np.ceil(16.0 * 8.0 ** ((np.arange(17, 32) - 16) / 16.0))]
SELF_AT = (0, 128, 384)
LOG2 = float(np.sqrt(2.0 / np.pi))
BLOCKS = ("wq", "wk", "wv", "wo", "ck", "cv", "cq", "co", "gt", "ut", "dn")
PLACE = {
    "wq": (0, 0, 768), "wk": (0, 768, 768), "cq": (0, 1536, 768), "ck": (0, 2304, 768),
    "wv": (1, 0, 768), "wo": (1, 768, 768), "cv": (1, 1536, 768), "co": (1, 2304, 768),
    "gt": (1, 3072, FF), "ut": (1, 5120, FF), "dn": (1, 7168, FF),
}


def f32(v):
    return v.astype(jnp.float32)


def half(v):
    return v.astype(jnp.bfloat16)


def dot_nn(a, b):
    return lax.dot_general(a, b, (((1,), (0,)), ((), ())), preferred_element_type=jnp.float32)


def dot_nt(a, b):
    return lax.dot_general(a, b, (((1,), (1,)), ((), ())), preferred_element_type=jnp.float32)


def dot_tn(a, b):
    return lax.dot_general(a, b, (((0,), (0,)), ((), ())), preferred_element_type=jnp.float32)


def lane_roll_rows(base, sign):
    rows = lax.broadcasted_iota(jnp.int32, base.shape, 0)
    for bit in range(3):
        step = (1 << bit) if sign > 0 else 256 - (1 << bit)
        base = jnp.where((rows >> bit) % 2 == 1, pltpu.roll(base, step, 1), base)
    return base


def layer_kernel(
    x, enc, cot, gains, table, seg, eseg, w_sc, w_wt,
    out, g_in, g_enc, g_sc, g_wt, g_gain, g_table,
    sc, wt, bias, smask, cmask, p1, p2, n1, q1, k1, v1, c1, y1, n2, q2, k2, v2, c2, y2, n3, cb,
    t1, t2, t3, dqs, dks, dvs, dk2s, dv2s, dn_acc, acc_k, acc_v, diag, hid, das, dbs, stage,
    w_sem, s_sem,
):
    vm = (sc, wt)
    hb = (w_sc, w_wt)
    copies = {}
    for i, name in enumerate(BLOCKS):
        array, first, rows = PLACE[name]
        copies[name] = pltpu.make_async_copy(
            hb[array].at[pl.ds(first, rows)], vm[array].at[pl.ds(first, rows)], w_sem.at[i]
        )
        copies[name].start()

    def weight(name):
        array, first, rows = PLACE[name]
        return vm[array].at[pl.ds(first, rows)]

    def need(*names):
        for name in names:
            copies[name].wait()

    def rows_loop(total, body, step=128):
        def run(i, carry):
            body(pl.ds(pl.multiple_of(i * step, step), step))
            return carry

        lax.fori_loop(0, total // step, run, 0)

    def cols_loop(total, body, step=CH):
        def run(i, carry):
            body(pl.ds(pl.multiple_of(i * step, step), step))
            return carry

        lax.fori_loop(0, total // step, run, 0)

    def rms_into(dst, src, row):
        def body(at):
            v = src[at, :]
            inv = lax.rsqrt(jnp.mean(v * v, axis=-1, keepdims=True) + EPSILON)
            dst[at, :] = half(v * inv * gains[row : row + 1, :])

        rows_loop(ROWS, body)

    def rms_back(dst, base, src, dn, row):
        g_gain[row : row + 1, :] = jnp.zeros((1, D), jnp.float32)

        def body(at):
            v = src[at, :]
            d = dn[at, :]
            inv = lax.rsqrt(jnp.mean(v * v, axis=-1, keepdims=True) + EPSILON)
            normed = v * inv
            g_gain[row : row + 1, :] += jnp.sum(d * normed, axis=0, keepdims=True)
            dg = d * gains[row : row + 1, :]
            dst[at, :] = base[at, :] + inv * (dg - normed * jnp.mean(dg * normed, axis=-1, keepdims=True))

        rows_loop(ROWS, body)

    def project(dst, src, name):
        w = weight(name)

        def body(at):
            dst[:, at] = half(dot_nn(src[...], w[:, at]))

        cols_loop(D, body)

    chunk_no = [0]

    def leave(value, array, first, slot, fresh):
        if not fresh:
            pltpu.make_async_copy(stage.at[slot], (g_sc, g_wt)[array].at[pl.ds(0, CH)], s_sem.at[slot]).wait()
        stage[slot] = half(value)
        pltpu.make_async_copy(
            stage.at[slot], (g_sc, g_wt)[array].at[pl.ds(pl.multiple_of(first, CH), CH)], s_sem.at[slot]
        ).start()

    def weight_grad(lhs, rhs, name):
        array, first, rows = PLACE[name]
        steps = rows // CH

        for i in range(steps):
            slot = chunk_no[0] % 3
            leave(dot_tn(lhs[:, i * CH : (i + 1) * CH], rhs[...]), array, first + i * CH, slot, chunk_no[0] < 3)
            chunk_no[0] += 1

    need("wq", "wk", "wv")
    distance = lax.broadcasted_iota(jnp.int32, (BUCKETS, SPAN), 1) - 128
    unit = lax.broadcasted_iota(jnp.int32, (BUCKETS, SPAN), 0)
    far = jnp.zeros_like(distance)
    for edge in BUCKET_EDGES:
        far = far + (distance >= edge).astype(jnp.int32)
    bucket = jnp.where(distance < 16, distance, 16 + far)
    one_hot = half((bucket == unit).astype(jnp.float32))
    row_bias = dot_nn(table[...], one_hot)
    row_bias = jnp.where(lax.broadcasted_iota(jnp.int32, (16, SPAN), 1) < 128, MASKED_SCORE, row_bias)
    diag[...] = row_bias

    def make_bias(h, carry):
        row = diag[pl.ds(h, 1), :]
        for delta in range(3):
            base = lane_roll_rows(
                jnp.broadcast_to(row[:, delta * 128 : delta * 128 + 256], (8, 256)), 1
            )
            for a in range(16):
                rolled = base if a == 0 else pltpu.roll(base, 8 * a, 1)
                bias[h, delta, a * 8 : a * 8 + 8, :] = rolled[:, 128:]
        return carry

    lax.fori_loop(0, H, make_bias, 0)
    seg_f = jnp.broadcast_to(f32(seg[...]), (ROWS, ROWS))
    smask[...] = jnp.where(seg_f.T == seg_f, 0.0, MASKED_SCORE)
    enc_f = jnp.broadcast_to(f32(eseg[...]), (128, KEYS)).T
    cmask[...] = jnp.where(
        jnp.concatenate([enc_f, enc_f, enc_f], axis=1) == jnp.broadcast_to(f32(seg[...]), (KEYS, ROWS)),
        0.0, MASKED_SCORE,
    )
    lanes_of = lax.broadcasted_iota(jnp.int32, (1, 128), 1) // 64

    def pick(v, e):
        return jnp.where(lanes_of == e, v, jnp.zeros_like(v))

    rms_into(n1, x, 0)
    project(q1, n1, "wq")
    project(k1, n1, "wk")
    project(v1, n1, "wv")

    def self_forward(pair, carry):
        lanes = pl.ds(pl.multiple_of(pair * 128, 128), 128)
        q = q1[:, lanes]
        k = k1[:, lanes]
        vt = v1[:, lanes].T
        tops = [[None, None] for _ in range(3)]
        for e in range(2):
            h = pair * 2 + e
            km = pick(k, e)
            for i in range(3):
                n = (i + 1) * 128
                s = dot_nt(km[:n], q[i * 128 : (i + 1) * 128])
                s = s + jnp.concatenate([bias[h, i - j] for j in range(i + 1)], axis=0)
                s = s + smask[:n, i * 128 : (i + 1) * 128]
                top = jnp.max(s, axis=0, keepdims=True)
                ex = jnp.exp(s - top)
                p = ex * (1.0 / jnp.sum(ex, axis=0, keepdims=True))
                p1[h, SELF_AT[i] : SELF_AT[i] + n, :] = p
                tops[i][e] = dot_nn(vt[e * 64 : (e + 1) * 64, :n], half(p))
        for i in range(3):
            c1[i * 128 : (i + 1) * 128, lanes] = half(jnp.concatenate(tops[i], axis=0).T)
        return carry

    lax.fori_loop(0, PAIRS, self_forward, 0)
    need("wo")

    def first_body(at):
        y1[:, at] = x[:, at] + dot_nn(c1[...], weight("wo")[:, at])

    cols_loop(D, first_body)

    rms_into(n2, y1, 1)
    need("cq", "ck", "cv")
    project(q2, n2, "cq")
    project(k2, enc, "ck")
    project(v2, enc, "cv")

    def cross_forward(pair, carry):
        lanes = pl.ds(pl.multiple_of(pair * 128, 128), 128)
        q = q2[:, lanes]
        k = k2[:, lanes]
        vt = v2[:, lanes].T
        tops = []
        for e in range(2):
            h = pair * 2 + e
            s = dot_nt(pick(k, e), q) + cmask[...]
            top = jnp.max(s, axis=0, keepdims=True)
            ex = jnp.exp(s - top)
            p = ex * (1.0 / jnp.sum(ex, axis=0, keepdims=True))
            p2[h] = p
            tops.append(dot_nn(vt[e * 64 : (e + 1) * 64, :], half(p)))
        c2[:, lanes] = half(jnp.concatenate(tops, axis=0).T)
        return carry

    lax.fori_loop(0, PAIRS, cross_forward, 0)
    need("co")

    def second_body(at):
        y2[:, at] = y1[:, at] + dot_nn(c2[...], weight("co")[:, at])

    cols_loop(D, second_body)

    rms_into(n3, y2, 2)

    def start_body(at):
        cb[at, :] = half(cot[at, :])
        out[at, :] = y2[at, :]
        dn_acc[at, :] = jnp.zeros((128, D), jnp.float32)

    rows_loop(ROWS, start_body)
    need("gt", "ut", "dn")
    gt, ut, dn = weight("gt"), weight("ut"), weight("dn")

    def ffn(i, carry):
        at = pl.ds(pl.multiple_of(i * CH, CH), CH)
        g_rows = gt[at, :]
        u_rows = ut[at, :]
        d_rows = dn[at, :]
        a = dot_nt(n3[...], g_rows)
        b = dot_nt(n3[...], u_rows)
        dh = dot_nt(cb[...], d_rows)
        inner = jnp.tanh(LOG2 * (a + 0.044715 * a * a * a))
        gelu = 0.5 * a * (1.0 + inner)
        slope = 0.5 * (1.0 + inner) + 0.5 * a * (1.0 - inner * inner) * (LOG2 * (1.0 + 3 * 0.044715 * a * a))
        hid[...] = half(gelu * b)
        das[...] = half(dh * b * slope)
        dbs[...] = half(dh * gelu)
        out[...] += dot_nn(hid[...], d_rows)
        dn_acc[...] += dot_nn(das[...], g_rows) + dot_nn(dbs[...], u_rows)
        for slot, (lhs, rhs, name) in enumerate(((hid, cb, "dn"), (das, n3, "gt"), (dbs, n3, "ut"))):
            array, first, _ = PLACE[name]

            @pl.when(i > 0)
            def _():
                pltpu.make_async_copy(stage.at[slot], g_wt.at[pl.ds(0, CH)], s_sem.at[slot]).wait()

            stage[slot] = half(dot_tn(lhs[...], rhs[...]))
            pltpu.make_async_copy(
                stage.at[slot], g_wt.at[pl.ds(pl.multiple_of(first + i * CH, CH), CH)], s_sem.at[slot]
            ).start()
        return carry

    lax.fori_loop(0, FF // CH, ffn, 0)
    chunk_no[0] = 24
    rms_back(t1, cot, y2, dn_acc, 2)

    def to_half_rows(dst, src):
        def body(at):
            dst[at, :] = half(src[at, :])

        rows_loop(ROWS, body)

    to_half_rows(cb, t1)
    weight_grad(c2, cb, "co")

    def back_project(dst, src, name):
        w = weight(name)

        def body(at):
            dst[:, at] = half(dot_nt(src[...], w[at, :]))

        cols_loop(D, body)

    back_project(t3, cb, "co")

    def cross_backward(pair, carry):
        lanes = pl.ds(pl.multiple_of(pair * 128, 128), 128)
        q = q2[:, lanes]
        k = k2[:, lanes]
        v = v2[:, lanes]
        do = t3[:, lanes]
        prod = (f32(do) * f32(c2[:, lanes])).T
        kt = k.T
        parts = []
        dk = dv = None
        for e in range(2):
            h = pair * 2 + e
            p = p2[h]
            dom = pick(do, e)
            delta = jnp.sum(prod[e * 64 : (e + 1) * 64], axis=0, keepdims=True)
            dv_e = dot_nn(half(p), dom)
            ds = half(p * (dot_nt(v, dom) - delta))
            dk_e = dot_nn(ds, pick(q, e))
            parts.append(dot_nn(kt[e * 64 : (e + 1) * 64, :], ds))
            dk = dk_e if dk is None else dk + dk_e
            dv = dv_e if dv is None else dv + dv_e
        dk2s[:, lanes] = half(dk)
        dv2s[:, lanes] = half(dv)
        dqs[:, lanes] = half(jnp.concatenate(parts, axis=0).T)
        return carry

    lax.fori_loop(0, PAIRS, cross_backward, 0)
    weight_grad(n2, dqs, "cq")
    weight_grad(enc, dk2s, "ck")
    weight_grad(enc, dv2s, "cv")
    ck, cv, cq = weight("ck"), weight("cv"), weight("cq")

    def enc_body(at):
        g_enc[:, at] = dot_nt(dk2s[...], ck[at, :]) + dot_nt(dv2s[...], cv[at, :])

    cols_loop(D, enc_body)

    def n2_body(at):
        dn_acc[:, at] = dot_nt(dqs[...], cq[at, :])

    cols_loop(D, n2_body)
    rms_back(t2, t1, y1, dn_acc, 1)

    to_half_rows(cb, t2)
    weight_grad(c1, cb, "wo")
    back_project(t3, cb, "wo")

    def self_backward(pair, carry):
        lanes = pl.ds(pl.multiple_of(pair * 128, 128), 128)
        k = k1[:, lanes]
        v = v1[:, lanes]
        kt = k.T
        diags = [[None] * 3, [None] * 3]
        for i in (2, 1, 0):
            n = (i + 1) * 128
            at = slice(i * 128, (i + 1) * 128)
            do = t3[at, lanes]
            q = q1[at, lanes]
            prod = (f32(do) * f32(c1[at, lanes])).T
            parts = []
            dk = dv = None
            for e in range(2):
                h = pair * 2 + e
                p = p1[h, SELF_AT[i] : SELF_AT[i] + n, :]
                dom = pick(do, e)
                delta = jnp.sum(prod[e * 64 : (e + 1) * 64], axis=0, keepdims=True)
                dv_e = dot_nn(half(p), dom)
                ds = p * (dot_nt(v[:n], dom) - delta)
                for j in range(i + 1):
                    piece = ds[j * 128 : (j + 1) * 128]
                    was = diags[e][i - j]
                    diags[e][i - j] = piece if was is None else was + piece
                w = half(ds)
                dk_e = dot_nn(w, pick(q, e))
                parts.append(dot_nn(kt[e * 64 : (e + 1) * 64, :n], w))
                dk = dk_e if dk is None else dk + dk_e
                dv = dv_e if dv is None else dv + dv_e
            if i == 2:
                acc_k[...] = dk
                acc_v[...] = dv
            else:
                acc_k[:n] += dk
                acc_v[:n] += dv
            dqs[at, lanes] = half(jnp.concatenate(parts, axis=0).T)
        dks[:, lanes] = half(acc_k[...])
        dvs[:, lanes] = half(acc_v[...])
        for e in range(2):
            sums = []
            for delta in range(3):
                block = diags[e][delta]
                wide = jnp.concatenate([jnp.zeros_like(block), block], axis=1)
                total = wide[0:8]
                for a in range(1, 16):
                    total = total + pltpu.roll(wide[a * 8 : a * 8 + 8], 256 - 8 * a, 1)
                sums.append(jnp.sum(lane_roll_rows(total, -1), axis=0, keepdims=True))
            zero = jnp.zeros((1, 128), jnp.float32)
            diag[pl.ds(pair * 2 + e, 1), :] = (
                jnp.concatenate([sums[0], zero, zero, zero], axis=1)
                + jnp.concatenate([zero, sums[1], zero, zero], axis=1)
                + jnp.concatenate([zero, zero, sums[2], zero], axis=1)
            )
        return carry

    diag[...] = jnp.zeros_like(diag)
    lax.fori_loop(0, PAIRS, self_backward, 0)
    weight_grad(n1, dqs, "wq")
    weight_grad(n1, dks, "wk")
    weight_grad(n1, dvs, "wv")
    rest = diag[...]
    total = jnp.zeros((16, BUCKETS), jnp.float32)
    for _ in range(3):
        top = half(rest)
        total = total + dot_nt(top, one_hot)
        rest = rest - f32(top)
    g_table[...] = total
    wq, wk, wv = weight("wq"), weight("wk"), weight("wv")

    def n1_body(at):
        dn_acc[:, at] = dot_nt(dqs[...], wq[at, :]) + dot_nt(dks[...], wk[at, :]) + dot_nt(dvs[...], wv[at, :])

    cols_loop(D, n1_body)
    rms_back(g_in, t2, x, dn_acc, 0)
    for slot in range(3):
        pltpu.make_async_copy(stage.at[slot], g_wt.at[pl.ds(0, CH)], s_sem.at[slot]).wait()


def layer(x, enc, cot, gains, table, seg, eseg, full_sc, full_wt):
    vmem = pl.BlockSpec(memory_space=pltpu.VMEM)
    hbm = pl.BlockSpec(memory_space=pl.ANY)
    bf, fl = jnp.bfloat16, jnp.float32
    wide = lambda kind: pltpu.VMEM((ROWS, D), kind)
    thin = lambda kind: pltpu.VMEM((KEYS, D), kind)
    return pl.pallas_call(
        layer_kernel,
        out_shape=(
            jax.ShapeDtypeStruct((ROWS, D), fl),
            jax.ShapeDtypeStruct((ROWS, D), fl),
            jax.ShapeDtypeStruct((KEYS, D), fl),
            jax.ShapeDtypeStruct((3072, D), bf),
            jax.ShapeDtypeStruct((9216, D), bf),
            jax.ShapeDtypeStruct((3, D), fl),
            jax.ShapeDtypeStruct((16, BUCKETS), fl),
        ),
        in_specs=[vmem] * 7 + [hbm] * 2,
        out_specs=(vmem, vmem, vmem, hbm, hbm, vmem, vmem),
        scratch_shapes=[
            pltpu.VMEM((3072, D), bf),
            pltpu.VMEM((9216, D), bf),
            pltpu.VMEM((H, 3, 128, 128), fl),
            pltpu.VMEM((ROWS, ROWS), fl),
            pltpu.VMEM((KEYS, ROWS), fl),
            pltpu.VMEM((H, 768, 128), fl),
            pltpu.VMEM((H, KEYS, ROWS), fl),
            wide(bf), wide(bf), wide(bf), wide(bf), wide(bf), wide(fl),
            wide(bf), wide(bf), thin(bf), thin(bf), wide(bf), wide(fl), wide(bf), wide(bf),
            wide(fl), wide(fl), wide(bf),
            wide(bf), wide(bf), wide(bf), thin(bf), thin(bf), wide(fl),
            pltpu.VMEM((ROWS, 128), fl), pltpu.VMEM((ROWS, 128), fl),
            pltpu.VMEM((16, SPAN), fl),
            pltpu.VMEM((ROWS, CH), bf), pltpu.VMEM((ROWS, CH), bf), pltpu.VMEM((ROWS, CH), bf),
            pltpu.VMEM((3, CH, D), bf),
            pltpu.SemaphoreType.DMA((len(BLOCKS),)),
            pltpu.SemaphoreType.DMA((3,)),
        ],
        compiler_params=pltpu.CompilerParams(vmem_limit_bytes=62 << 20),
        name="layer",
    )(x, enc, cot, gains, table, seg, eseg, full_sc, full_wt)


def per_device(inputs, encoded, cotangent, scoring, weights, small_params, dec_segments, enc_segments):
    full_sc, full_wt, full_small = gather_params(scoring, weights, small_params)
    gains = full_small[: 3 * D].astype(jnp.float32).reshape(3, D)
    table = jnp.pad(full_small[3 * D :].reshape(BUCKETS, H).T, ((0, 4), (0, 0)))
    out, g_in, g_enc, g_sc, g_wt, g_gain, g_table = layer(
        inputs, encoded, cotangent, gains, table, dec_segments, enc_segments, full_sc, full_wt
    )
    g_small = jnp.concatenate([g_gain.reshape(-1), g_table[:H].T.reshape(-1)])
    o_sc, o_wt, o_sm = scatter_grads(g_sc, g_wt, g_small)
    return out, g_in, g_enc, o_sc, o_wt, o_sm


def solution(mesh):
    rows = P(("dp", "fsdp"), None)
    flat = P(("dp", "fsdp"))
    return jax.shard_map(
        per_device,
        mesh=mesh,
        in_specs=(rows, rows, rows, rows, rows, flat, rows, rows),
        out_specs=(rows, rows, rows, rows, rows, flat),
        check_vma=False,
    )
```
